512 devices in a mesh: ctx: 16 (over y, x_hi, core), fsdp: 32 (over z, x_lo).
Axes of the slice: x: 4 (x_hi: 2, x_lo: 2; x = x_hi * 2 + x_lo), y: 4, z: 16, core: 2. Of those that a mesh axis runs over, the one named last changes fastest.
Arguments:
- query_states: bfloat16 [32, 2048, 2048], P('fsdp', 'ctx'), may hold values from -12 to 12
- key_states: bfloat16 [32, 2048, 512], P('fsdp', 'ctx'), may hold values from -24 to 24
- value_states: bfloat16 [32, 2048, 512], P('fsdp', 'ctx'), may hold values from -170 to 170
- doc_ids: int32 [32, 2048], P('fsdp', 'ctx'), may hold values from 0 to 7, never falling along the last dimension, each value on 1 to 1536 neighbouring positions
- routes: int32 [32, 2048, 2], P('fsdp', 'ctx'), may hold values from 0 to 7, as said below
- route_weight: bfloat16 [32, 2048, 2], P('fsdp', 'ctx'), may hold values from 0.19921875 to 1
- cotangent: bfloat16 [32, 2048, 2048], P('fsdp', 'ctx'), may hold values from -6 to 6
- gate_weight: bfloat16 [2048, 7168], P('fsdp', 'ctx'), may hold values from -0.125 to 0.125
- up_weight: bfloat16 [2048, 7168], P('fsdp', 'ctx'), may hold values from -0.125 to 0.125
- down_weight: bfloat16 [7168, 2048], P('ctx', 'fsdp'), may hold values from -0.0625 to 0.0625
Outputs:
- attn_out: bfloat16 [32, 2048, 2048], P('fsdp', 'ctx')
- d_input: bfloat16 [32, 2048, 2048], P('fsdp', 'ctx')
The draws below stay inside these ranges and needn't reach their ends.
Inputs may be any that keep to these rules, and one draw needn't show every extreme that they name: `routes`: each token names 2 different experts. Of the 128 tokens of one block of a sequence, at most 8 name expert 0; in some sequence every block has exactly 8 such tokens.
All inputs are finite; a program needn't handle non-finite values.
Results may differ from the reference program's by a relative error of at most 0.02.
Values may be sent and summed in bfloat16 or wider, within the bound.
No kernel may reach another device: no remote copies, remote signals or barrier semaphores. Data moves between devices by JAX's collectives and lax.ppermute only.
A program may use at most 64 MiB of HBM per device.

```python
import math
import jax
import jax.numpy as jnp
import numpy as np
from jax import lax

HEADS = 16
KV_HEADS = 4
HEAD_DIM = 128
FF = 7168
EXPERTS = 8
TOP = 2
TOK_DEV = 128
D = 2048
CAP = 8
LENGTH = 2048
SEQS = 32
N_CTX = 16


def draw_key_states(key, part):
    noise = jnp.clip(jax.random.normal(jax.random.fold_in(key, 21), (SEQS, LENGTH, KV_HEADS, HEAD_DIM), jnp.float32), -4.0, 4.0)
    return noise.reshape(SEQS, LENGTH, KV_HEADS * HEAD_DIM).astype(jnp.bfloat16)


def draw_query_states(key, part):
    noise = jnp.clip(jax.random.normal(jax.random.fold_in(key, 31), (SEQS, LENGTH, HEADS, HEAD_DIM), jnp.float32), -4.0, 4.0)
    return noise.reshape(SEQS, LENGTH, HEADS * HEAD_DIM).astype(jnp.bfloat16)


def draw_value_states(key, part):
    base_key = jax.random.fold_in(jax.random.fold_in(key, 41), 0)
    shape_all = (SEQS, LENGTH, KV_HEADS * HEAD_DIM)
    result = jnp.clip(jax.random.normal(base_key, shape_all, jnp.float32), -4.0, 4.0)
    return result.astype(jnp.bfloat16)


def draw_routes(key, part):
    blocks = LENGTH // TOK_DEV
    key_list = jax.random.split(jax.random.fold_in(key, 51), 6)
    block_shape = (SEQS, blocks, TOK_DEV)
    counts = jax.random.randint(key_list[0], (SEQS, blocks), CAP // 4, CAP + 1)
    full_sequence = jax.random.randint(key_list[1], (), 0, SEQS)
    counts = jnp.where(jnp.arange(SEQS)[:, None] == full_sequence, CAP, counts)
    scores = jax.random.randint(key_list[2], block_shape, 0, 65536) * TOK_DEV + jnp.arange(TOK_DEV)
    rank_order = jnp.argsort(jnp.argsort(scores, axis=-1, stable=True), axis=-1, stable=True)
    chosen = rank_order < counts[..., None]
    first_pick = jax.random.randint(key_list[3], block_shape, 1, EXPERTS)
    second_pick = 1 + (first_pick - 1 + jax.random.randint(key_list[4], block_shape, 1, EXPERTS - 1)) % (EXPERTS - 1)
    flip_order = jax.random.randint(key_list[5], block_shape, 0, 2) == 1
    column_one = jnp.where(chosen, jnp.where(flip_order, first_pick, 0), first_pick)
    column_two = jnp.where(chosen, jnp.where(flip_order, 0, first_pick), second_pick)
    stacked = jnp.stack([column_one, column_two], axis=-1)
    return stacked.reshape(SEQS, LENGTH, TOP).astype(jnp.int32)


def block_scale(rng, shape, cuts, smallest, high):
    loudness, own = 1.0, jax.random.fold_in(rng, 6)
    for position, shards_of in cuts:
        heights = jnp.exp(jax.random.uniform(jax.random.fold_in(own, position), (shards_of,), jnp.float32, smallest / len(cuts), high / len(cuts)))
        loudness = loudness * jnp.repeat(heights, shape[position] // shards_of).reshape([-1 if axis == position else 1 for axis in range(len(shape))])
    return loudness


def profile(number_of, total, reach, skew):
    weights = [(1 << 20) // math.isqrt(rank ** skew) + 1 for rank in range(2, number_of + 1)]
    spare, given = total - reach - (number_of - 1), [1] * (number_of - 1)
    while spare > 0:
        free = [i for i in range(number_of - 1) if given[i] < reach]
        mass, left = sum([weights[i] for i in free]), spare
        for i in free:
            more = min(reach - given[i], max(1, left * weights[i] // mass), spare)
            given[i] = given[i] + more
            spare = spare - more
    return np.array([reach] + given)


def uneven_parts(own_key, count, total, limit, slope):
    if count == 2:
        one = jax.random.randint(own_key, (), max(1, total - limit), min(limit, total - 1) + 1)
        return jnp.stack([one, total - one])
    tallies = jnp.asarray(profile(count, total, limit, slope), jnp.int32)
    couples = (count - 1) // 2
    source_of, taker = tallies[1:1 + 2 * couples:2], tallies[2:2 + 2 * couples:2]
    room = jnp.minimum(source_of - 1, limit - taker)
    moved = jax.random.randint(jax.random.fold_in(own_key, 1), (couples,), 0, 1 << 20) % (room + 1)
    tallies = tallies.at[1:1 + 2 * couples:2].set(source_of - moved).at[2:2 + 2 * couples:2].set(taker + moved)
    return tallies[jax.random.permutation(jax.random.fold_in(own_key, 2), count)]


def bell_draw(stream_key, shape, width, most, cuts=(), dtype=jnp.bfloat16):
    factor_of = block_scale(stream_key, shape, cuts, -0.22, 0.18) if cuts else 1.0
    values = jax.random.normal(stream_key, shape, jnp.float32) * width * factor_of
    return jnp.minimum(jnp.maximum(values, -most), most).astype(dtype)


def setup_inputs(seed: int = 0) -> dict:
    arg_keys = jax.random.split(jax.random.key(seed), 11)
    query_states = draw_query_states(jax.random.fold_in(arg_keys[10], 71), 0)
    key_states = draw_key_states(jax.random.fold_in(arg_keys[10], 71), 0)
    value_states = draw_value_states(jax.random.fold_in(arg_keys[10], 71), 0)
    doc_ids = jax.vmap(lambda own: jnp.searchsorted(jnp.cumsum(uneven_parts(own, 8, LENGTH, LENGTH * 3 // 4, 1)), jnp.arange(LENGTH), side="right"))(jax.random.split(arg_keys[3], SEQS)).reshape((SEQS, LENGTH)).astype(jnp.int32)
    routes = draw_routes(jax.random.fold_in(arg_keys[10], 71), 0)
    route_weight = jnp.clip(0.19921875 + 0.80078125 * jax.random.uniform(arg_keys[5], (SEQS, LENGTH, TOP), jnp.float32) ** block_scale(arg_keys[5], (SEQS, LENGTH, TOP), ((0, 32), (1, 16)), -0.2, 0.2), 0.19921875, 1.0).astype(jnp.bfloat16)
    cotangent = bell_draw(arg_keys[6], (SEQS, LENGTH, D), 1.0, 6.0, ((0, 32), (1, 16)))
    gate_weight = bell_draw(arg_keys[7], (D, FF), D ** -0.5, 0.125, ((0, 32), (1, 16)))
    up_weight = bell_draw(arg_keys[8], (D, FF), D ** -0.5, 0.125, ((0, 32), (1, 16)))
    down_weight = bell_draw(arg_keys[9], (FF, D), FF ** -0.5, 0.0625, ((0, 16), (1, 32)))
    return {"query_states": query_states, "key_states": key_states, "value_states": value_states, "doc_ids": doc_ids, "routes": routes, "route_weight": route_weight, "cotangent": cotangent, "gate_weight": gate_weight, "up_weight": up_weight, "down_weight": down_weight}


epsilon = 1e-05
far_below = -1e+30

def attend_sequence(operands):
    query_states, key_states, value_states, doc_ids = operands
    group_size = HEADS // KV_HEADS
    query_heads = jnp.transpose(query_states.reshape(LENGTH, KV_HEADS, group_size, HEAD_DIM), (1, 0, 2, 3))
    key_heads = jnp.transpose(key_states.reshape(LENGTH, KV_HEADS, HEAD_DIM), (1, 0, 2))
    value_heads = jnp.transpose(value_states.reshape(LENGTH, KV_HEADS, HEAD_DIM), (1, 0, 2))
    allowed = doc_ids[None, :] == doc_ids[:, None]

    def one_head(parts):
        query_one, key_one, value_one = parts
        scores = jnp.einsum('ird,jd->rij', query_one.astype(jnp.float32), key_one.astype(jnp.float32)) * HEAD_DIM ** (-0.5)
        masked = jnp.where(allowed, scores, far_below)
        row_max = lax.optimization_barrier(jnp.max(masked, axis=-1, keepdims=True))
        unscaled = jnp.where(allowed, jnp.exp(masked - row_max), 0.0)
        row_total = lax.optimization_barrier(jnp.sum(unscaled, axis=-1))
        probabilities = lax.optimization_barrier(unscaled.astype(jnp.bfloat16)).astype(jnp.float32)
        mixed = jnp.einsum('rij,jd->rid', probabilities, value_one.astype(jnp.float32))
        return mixed / row_total[..., None]
    mixed = lax.map(one_head, (query_heads, key_heads, value_heads))
    return jnp.transpose(mixed, (2, 0, 1, 3)).reshape(LENGTH, D).astype(jnp.bfloat16)

def reference(query_states, key_states, value_states, doc_ids, routes, route_weight, cotangent, gate_weight, up_weight, down_weight):
    attn_out = lax.map(attend_sequence, (query_states, key_states, value_states, doc_ids))
    as_float = attn_out.astype(jnp.float32)
    inverse = lax.rsqrt(lax.optimization_barrier(jnp.mean(as_float * as_float, axis=-1, keepdims=True)) + epsilon)
    scaled = as_float * inverse
    normed = scaled.astype(jnp.bfloat16)
    chosen = routes == 0
    routed = jnp.any(chosen, axis=-1).reshape(SEQS, N_CTX, TOK_DEV)
    weight = lax.optimization_barrier(jnp.sum(jnp.where(chosen, route_weight.astype(jnp.float32), 0.0), axis=-1)).reshape(SEQS, N_CTX, TOK_DEV)
    slot_index = jnp.cumsum(routed.astype(jnp.int32), axis=-1) - 1
    selector = ((slot_index[:, :, None, :] == jnp.arange(CAP)[:, None]) & routed[:, :, None, :]).astype(jnp.float32)
    highest = lax.Precision.HIGHEST
    packed_x = jnp.einsum('snct,sntd->sncd', selector, normed.astype(jnp.float32).reshape(SEQS, N_CTX, TOK_DEV, D), precision=highest)
    packed_dy = jnp.einsum('snct,sntd->sncd', selector, cotangent.astype(jnp.float32).reshape(SEQS, N_CTX, TOK_DEV, D), precision=highest)
    packed_w = jnp.einsum('snct,snt->snc', selector, weight, precision=highest)
    packed_x = packed_x.astype(jnp.bfloat16).reshape(SEQS, N_CTX * CAP, D)
    packed_dy = packed_dy.astype(jnp.bfloat16).reshape(SEQS, N_CTX * CAP, D)
    packed_w = packed_w.reshape(SEQS, N_CTX * CAP)
    hidden_share = FF // N_CTX

    def expert_rows(operands):
        rows_x, rows_dy, rows_w = operands
        row_count = rows_x.shape[0]
        gate_proj = jnp.dot(rows_x, gate_weight, preferred_element_type=jnp.float32)
        up_proj = jnp.dot(rows_x, up_weight, preferred_element_type=jnp.float32)
        back_grad = jnp.dot(rows_dy, down_weight.T, preferred_element_type=jnp.float32) * rows_w[:, None]
        sigmoid_gate = jax.nn.sigmoid(gate_proj)
        grad_gate = (back_grad * up_proj * sigmoid_gate * (1.0 + gate_proj * (1.0 - sigmoid_gate))).astype(jnp.bfloat16)
        grad_up = (back_grad * gate_proj * sigmoid_gate).astype(jnp.bfloat16)
        gate_groups = gate_weight.astype(jnp.float32).reshape(D, N_CTX, hidden_share)
        up_groups = up_weight.astype(jnp.float32).reshape(D, N_CTX, hidden_share)
        partial_terms = jnp.einsum('rcf,dcf->crd', grad_gate.astype(jnp.float32).reshape(row_count, N_CTX, hidden_share), gate_groups, precision=highest)
        partial_terms = partial_terms + jnp.einsum('rcf,dcf->crd', grad_up.astype(jnp.float32).reshape(row_count, N_CTX, hidden_share), up_groups, precision=highest)
        rounded = lax.optimization_barrier(partial_terms.astype(jnp.bfloat16)).astype(jnp.float32)
        return lax.optimization_barrier(jnp.sum(rounded, axis=0))
    d_slots = lax.map(expert_rows, (packed_x, packed_dy, packed_w)).reshape(SEQS, N_CTX, CAP, D)
    d_norm = jnp.einsum('snct,sncd->sntd', selector, d_slots, precision=highest).reshape(SEQS, LENGTH, D)
    d_input = inverse * (d_norm - scaled * lax.optimization_barrier(jnp.mean(d_norm * scaled, axis=-1, keepdims=True)))
    return (attn_out, d_input.astype(jnp.bfloat16))
```

```python
import jax
import jax.numpy as jnp
from jax import lax
from jax.experimental import pallas as pl
from jax.experimental.pallas import tpu as pltpu
from jax.sharding import Mesh
from jax.sharding import PartitionSpec as P

HEADS = 16
KV_HEADS = 4
HEAD_DIM = 128
CAP = 8
TOK = 128
D = 2048
DOCS = 8
EPS = 1e-05
LOG2E = 1.4426950408889634
QW = HEADS * HEAD_DIM // 2
KW = KV_HEADS * HEAD_DIM // 2
ROWS = TOK + 8
FAR = -(2.0**20)
PAY = 2 * D + 128
HALF = 256
F32, BF16 = jnp.float32, jnp.bfloat16
CHIPS = ("y", "xh")
PEERS = ("y", "xh", "xl")
CTX = ("y", "xh", "core")
FSDP = ("z", "xl")
NT = (((1,), (1,)), ((), ()))
TN = (((0,), (0,)), ((), ()))


def call(kernel, out_shape, *operands, flops=0, smem=0, **kw):
    nbytes = sum(o.size * o.dtype.itemsize for o in operands)
    nbytes += sum(o.size * o.dtype.itemsize for o in jax.tree.leaves(out_shape))
    vmem = pl.BlockSpec(memory_space=pltpu.VMEM)
    specs = [pl.BlockSpec(memory_space=pltpu.SMEM)] * smem + [vmem] * (len(operands) - smem)
    return pl.pallas_call(
        kernel,
        out_shape=out_shape,
        in_specs=specs,
        out_specs=jax.tree.map(lambda _: vmem, out_shape),
        cost_estimate=pl.CostEstimate(flops=flops, bytes_accessed=nbytes, transcendentals=0),
        **kw,
    )(*operands)


def pack_weights(gate_ref, up_ref, down_ref, out_ref):
    rows = gate_ref.shape[0]
    ff = gate_ref.shape[1]
    rest = ff - HALF
    eye = lax.broadcasted_iota(jnp.int32, (rows, rows), 0) == lax.broadcasted_iota(
        jnp.int32, (rows, rows), 1
    )
    down = lax.dot_general(
        eye.astype(BF16), down_ref[...], NT, preferred_element_type=F32
    ).astype(BF16)
    for i, full in enumerate((gate_ref[...], up_ref[...], down)):
        here = slice(i * rows, (i + 1) * rows)
        out_ref[0, here, :] = full[:, :HALF]
        out_ref[1, here, :] = jnp.concatenate(
            [full[:, HALF:], jnp.zeros((rows, HALF - rest), BF16)], axis=1
        )


def pack_heads(q_ref, k_ref, v_ref, doc_ref, out_ref):
    docs = jnp.broadcast_to(doc_ref[...].astype(F32), (8, TOK)).astype(BF16)
    for c in range(2):
        out_ref[c, :TOK, :QW] = q_ref[0, :, c * QW : (c + 1) * QW]
        out_ref[c, :TOK, QW : QW + KW] = k_ref[0, :, c * KW : (c + 1) * KW]
        out_ref[c, :TOK, QW + KW :] = v_ref[0, :, c * KW : (c + 1) * KW]
        out_ref[c, TOK:, :] = jnp.zeros((8, QW + 2 * KW), BF16)
        out_ref[c, TOK:, QW : QW + TOK] = docs


def attend(base_ref, q_ref, kv_ref, out_ref, k_aug, v_aug):
    length = k_aug.shape[1]
    docs = kv_ref[:, TOK:, :TOK].astype(F32)
    lane = lax.broadcasted_iota(jnp.int32, (1, 128), 1)
    first = jnp.zeros((1, 128), F32)
    after = jnp.where(lane < DOCS, float(length), 0.0)
    for d in range(1, DOCS):
        below = jnp.sum(jnp.where(docs < float(d), 1.0, 0.0), axis=0)
        count = jnp.sum(below[:1], axis=1, keepdims=True)
        first = jnp.where(lane == d, count, first)
        after = jnp.where(lane == d - 1, count, after)
    spot = lax.broadcasted_iota(jnp.int32, (length, 128), 0).astype(F32)
    inside = (spot >= first) & (spot < after)
    k_doc = jnp.where(inside, 0.0, FAR).astype(BF16)
    for g in range(2):
        here = slice(g * HEAD_DIM, (g + 1) * HEAD_DIM)
        there = slice(KW + g * HEAD_DIM, KW + (g + 1) * HEAD_DIM)
        k_aug[g, :, :HEAD_DIM] = kv_ref[:, :TOK, here].reshape(length, HEAD_DIM)
        k_aug[g, :, HEAD_DIM:] = k_doc
        v_aug[g, :, :HEAD_DIM] = kv_ref[:, :TOK, there].reshape(length, HEAD_DIM)
        v_aug[g, :, HEAD_DIM:] = jnp.ones((length, HEAD_DIM), BF16)
    mine = (lax.broadcasted_iota(jnp.int32, (2 * TOK, 128), 0) + base_ref[0, 0]).astype(F32)
    q_doc = jnp.where((mine >= first) & (mine < after), 1.0, 0.0).astype(BF16)
    factor = HEAD_DIM**-0.5 * LOG2E
    for h in range(HEADS // 2):
        g = h // (HEADS // KV_HEADS)
        here = slice(h * HEAD_DIM, (h + 1) * HEAD_DIM)
        q = q_ref[:, :TOK, here].reshape(2 * TOK, HEAD_DIM)
        q = jnp.concatenate([q, q_doc], axis=1)
        scores = lax.dot_general(q, k_aug[g], NT, preferred_element_type=F32)
        top = jnp.max(scores, axis=1, keepdims=True)
        probs = jnp.exp2((scores - top) * factor).astype(BF16)
        mixed = jnp.dot(probs, v_aug[g], preferred_element_type=F32)
        mixed = (mixed[:, :HEAD_DIM] / mixed[:, HEAD_DIM:]).astype(BF16)
        out_ref[:, :, here] = mixed.reshape(2, TOK, HEAD_DIM)


def selection(route_ref, width):
    chosen = route_ref[0] == 0
    routed = jnp.max(jnp.where(chosen, 1.0, 0.0), axis=1, keepdims=True)
    rows = lax.broadcasted_iota(jnp.int32, (TOK, TOK), 0)
    cols = lax.broadcasted_iota(jnp.int32, (TOK, TOK), 1)
    upto = (cols <= rows).astype(F32).astype(BF16)
    wide = jnp.broadcast_to(routed, (TOK, 128)).astype(BF16)
    slot = jnp.dot(upto, wide, preferred_element_type=F32) - 1.0
    lane = cols.astype(F32)
    hit = (slot == lane) & (lane < float(CAP))
    if width == 2:
        hit = hit | ((slot + float(CAP) == lane) & (slot < float(CAP)))
    return jnp.where(hit & (routed > 0.5), 1.0, 0.0), chosen


def normalized(attn):
    square = jnp.mean(attn * attn, axis=1, keepdims=True)
    inverse = lax.rsqrt(square + EPS)
    return inverse, attn * inverse


def send_slots(mixed_ref, route_ref, rw_ref, cot_ref, attn_ref, pay_ref):
    for c in range(2):
        attn_ref[0, :, c * QW : (c + 1) * QW] = mixed_ref[c]
    _, scaled = normalized(attn_ref[0].astype(F32))
    select, chosen = selection(route_ref, 1)
    select = select.astype(BF16)
    weight = jnp.sum(jnp.where(chosen, rw_ref[0].astype(F32), 0.0), axis=1, keepdims=True)
    weight = jnp.broadcast_to(weight, (TOK, 128)).astype(BF16)

    def take(rows):
        got = lax.dot_general(select, rows, TN, preferred_element_type=F32)
        return got[:CAP].astype(BF16)

    x, dy, w = take(scaled.astype(BF16)), take(cot_ref[0]), take(weight)
    for i in range(pay_ref.shape[0] // CAP):
        here = slice(i * CAP, (i + 1) * CAP)
        pay_ref[here, :D] = x
        pay_ref[here, D : 2 * D] = dy
        pay_ref[here, 2 * D :] = w


def expert(own_ref, other_ref, w_ref, own_out, other_out):
    def panel(i):
        return w_ref[:, i * 64 : (i + 1) * 64, :].reshape(D, HALF)

    gate_w, up_w, down_w = panel(0), panel(1), panel(2)
    for ref, out in ((own_ref, own_out), (other_ref, other_out)):
        x, dy = ref[:, :D], ref[:, D : 2 * D]
        gate = jnp.dot(x, gate_w, preferred_element_type=F32)
        up = jnp.dot(x, up_w, preferred_element_type=F32)
        back = jnp.dot(dy, down_w, preferred_element_type=F32)
        back = back * ref[:, 2 * D : 2 * D + 1].astype(F32)
        sg = jax.nn.sigmoid(gate)
        grad_gate = (back * up * sg * (1.0 + gate * (1.0 - sg))).astype(BF16)
        grad_up = (back * gate * sg).astype(BF16)
        part = lax.dot_general(grad_gate, gate_w, NT, preferred_element_type=F32)
        part = part + lax.dot_general(grad_up, up_w, NT, preferred_element_type=F32)
        out[...] = part.astype(out.dtype)


def finish(attn_ref, route_ref, part_ref, out_ref):
    total = part_ref[0].astype(F32)
    for i in range(1, part_ref.shape[0]):
        total = total + part_ref[i].astype(F32)
    high = total.astype(BF16)
    low = (total - high.astype(F32)).astype(BF16)
    inverse, scaled = normalized(attn_ref[0].astype(F32))
    select, _ = selection(route_ref, 2)
    pair = jnp.concatenate([high.astype(F32), low.astype(F32)], axis=0).astype(BF16)
    d_norm = jnp.dot(
        select[:, : 2 * CAP].astype(BF16), pair, preferred_element_type=F32
    )
    mean = jnp.mean(d_norm * scaled, axis=1, keepdims=True)
    out_ref[0] = (inverse * (d_norm - scaled * mean)).astype(BF16)


def all_to_all(x, axes):
    return lax.all_to_all(x, axes, 0, 0, tiled=True)


def swap_cores(x):
    return lax.ppermute(x, "core", [(0, 1), (1, 0)])


def on_device(q, k, v, doc_ids, routes, route_weight, cotangent, gate_w, up_w, down_w):
    shape = jax.ShapeDtypeStruct
    rows = gate_w.shape[0]
    halves = call(pack_weights, shape((2, 3 * rows, HALF), BF16), gate_w, up_w, down_w)
    halves = all_to_all(halves.reshape(6 * rows, HALF), "xl")
    panels = lax.all_gather(halves, "z", axis=0, tiled=True)
    panels = panels.reshape(-1, 3 * rows, HALF)

    width = QW + 2 * KW
    packed = call(pack_heads, shape((2, ROWS, width), BF16), q, k, v, doc_ids)
    packed = all_to_all(packed.reshape(2 * ROWS, width), "core")
    chips = lax.axis_size(CHIPS)
    kv = jnp.broadcast_to(packed[None, :, QW:], (chips, 2 * ROWS, 2 * KW))
    kv = all_to_all(kv.reshape(chips * 2 * ROWS, 2 * KW), CHIPS).reshape(-1, ROWS, 2 * KW)
    length = kv.shape[0] * TOK
    base = (lax.axis_index(CHIPS) * (2 * TOK)).astype(jnp.int32).reshape(1, 1)
    mixed = call(
        attend,
        shape((2, TOK, QW), BF16),
        base,
        packed.reshape(2, ROWS, width),
        kv,
        smem=1,
        flops=16 * TOK * length * QW,
        scratch_shapes=[pltpu.VMEM((2, length, 2 * HEAD_DIM), BF16)] * 2,
    )
    mixed = all_to_all(mixed.reshape(2 * TOK, QW), "core").reshape(2, TOK, QW)
    peers = lax.axis_size(PEERS)
    attn, pay = call(
        send_slots,
        (shape((1, TOK, D), BF16), shape((peers * CAP, PAY), BF16)),
        mixed,
        routes,
        route_weight,
        cotangent,
    )
    own = all_to_all(pay, PEERS)
    other = swap_cores(own)
    own_part, other_part = call(
        expert,
        (shape((peers * CAP, D), F32), shape((peers * CAP, D), BF16)),
        own,
        other,
        panels,
        flops=20 * peers * CAP * D * HALF,
    )
    part = (own_part + swap_cores(other_part).astype(F32)).astype(BF16)
    part = all_to_all(part, PEERS).reshape(peers, CAP, D)
    d_input = call(finish, shape((1, TOK, D), BF16), attn, routes, part)
    return attn, d_input


def solution(mesh):
    fine = Mesh(mesh.devices.reshape(4, 2, 2, 16, 2), ("y", "xh", "core", "z", "xl"))
    return jax.shard_map(
        on_device,
        mesh=fine,
        in_specs=(
            P(FSDP, CTX, None),
            P(FSDP, CTX, None),
            P(FSDP, CTX, None),
            P(FSDP, CTX),
            P(FSDP, CTX, None),
            P(FSDP, CTX, None),
            P(FSDP, CTX, None),
            P(FSDP, CTX),
            P(FSDP, CTX),
            P(CTX, FSDP),
        ),
        out_specs=(P(FSDP, CTX, None), P(FSDP, CTX, None)),
        check_vma=False,
    )
```

```python
import jax
import jax.numpy as jnp
from jax import lax
from jax.experimental import pallas as pl
from jax.experimental.pallas import tpu as pltpu
from jax.sharding import Mesh
from jax.sharding import PartitionSpec as P

HEADS = 16
KV_HEADS = 4
HEAD_DIM = 128
CAP = 8
TOK = 128
D = 2048
DOCS = 8
EPS = 1e-05
LOG2E = 1.4426950408889634
QW = HEADS * HEAD_DIM // 2
KW = KV_HEADS * HEAD_DIM // 2
FAR = -(2.0**20)
HALF = 256
F32, BF16 = jnp.float32, jnp.bfloat16
CHIPS = ("y", "xh")
PEERS = ("y", "xh", "xl")
CTX = ("y", "xh", "core")
FSDP = ("z", "xl")
NT = (((1,), (1,)), ((), ()))
TN = (((0,), (0,)), ((), ()))


def call(kernel, out_shape, *operands, flops=0, smem=0, hbm=0, **kw):
    nbytes = sum(o.size * o.dtype.itemsize for o in operands)
    nbytes += sum(o.size * o.dtype.itemsize for o in jax.tree.leaves(out_shape))
    vmem = pl.BlockSpec(memory_space=pltpu.VMEM)
    specs = [pl.BlockSpec(memory_space=pltpu.SMEM)] * smem
    specs += [vmem] * (len(operands) - smem - hbm)
    specs += [pl.BlockSpec(memory_space=pl.ANY)] * hbm
    return pl.pallas_call(
        kernel,
        out_shape=out_shape,
        in_specs=specs,
        out_specs=jax.tree.map(lambda _: vmem, out_shape),
        cost_estimate=pl.CostEstimate(flops=flops, bytes_accessed=nbytes, transcendentals=0),
        **kw,
    )(*operands)


def pack_weights(side_ref, gate_ref, up_ref, down_ref, keep_ref, send_ref):
    rows = gate_ref.shape[0]
    rest = gate_ref.shape[1] - HALF

    def write(low_ref, high_ref):
        for i, ref in enumerate((gate_ref, up_ref, down_ref)):
            here = slice(i * rows, (i + 1) * rows)
            low_ref[here, :] = ref[:, :HALF]
            high_ref[here, :] = jnp.concatenate(
                [ref[:, HALF:], jnp.zeros((rows, HALF - rest), BF16)], axis=1
            )

    @pl.when(side_ref[0, 0] == 0)
    def _():
        write(keep_ref, send_ref)

    @pl.when(side_ref[0, 0] != 0)
    def _():
        write(send_ref, keep_ref)


def pack_heads(core_ref, q_ref, k_ref, v_ref, doc_ref, keep_ref, send_ref):
    docs = jnp.broadcast_to(doc_ref[...].astype(F32), (8, TOK)).astype(BF16)
    core = core_ref[0, 0]
    for side, out_ref in ((core, keep_ref), (1 - core, send_ref)):
        row = 0
        for ref, width in ((q_ref, QW), (k_ref, KW), (v_ref, KW)):
            for h in range(width // HEAD_DIM):
                start = pl.multiple_of(side * width + h * HEAD_DIM, HEAD_DIM)
                out_ref[row : row + TOK, :] = ref[0, :, pl.ds(start, HEAD_DIM)]
                row += TOK
        out_ref[row:, :] = docs


def attend(base_ref, own_ref, other_ref, kv_ref, keep_ref, send_ref, k_aug, v_aug):
    length = k_aug.shape[1]
    heads = KW // HEAD_DIM
    docs = kv_ref[:, 2 * heads * TOK :, :].astype(F32)
    lane = lax.broadcasted_iota(jnp.int32, (1, 128), 1)
    first = jnp.zeros((1, 128), F32)
    after = jnp.where(lane < DOCS, float(length), 0.0)
    for d in range(1, DOCS):
        below = jnp.sum(jnp.where(docs < float(d), 1.0, 0.0), axis=0)
        count = jnp.sum(below[:1], axis=1, keepdims=True)
        first = jnp.where(lane == d, count, first)
        after = jnp.where(lane == d - 1, count, after)
    turn = base_ref[0, 1]
    spot = (lax.broadcasted_iota(jnp.int32, (length, 128), 0) ^ turn).astype(F32)
    inside = (spot >= first) & (spot < after)
    k_doc = jnp.where(inside, 0.0, FAR).astype(BF16)
    for g in range(heads):
        here = slice(g * TOK, (g + 1) * TOK)
        there = slice((heads + g) * TOK, (heads + g + 1) * TOK)
        k_aug[g, :, :HEAD_DIM] = kv_ref[:, here, :].reshape(length, HEAD_DIM)
        k_aug[g, :, HEAD_DIM:] = k_doc
        v_aug[g, :, :HEAD_DIM] = kv_ref[:, there, :].reshape(length, HEAD_DIM)
        v_aug[g, :, HEAD_DIM:] = jnp.ones((length, HEAD_DIM), BF16)
    mine = lax.broadcasted_iota(jnp.int32, (2 * TOK, 128), 0) ^ turn
    mine = (mine + base_ref[0, 0]).astype(F32)
    q_doc = jnp.where((mine >= first) & (mine < after), 1.0, 0.0).astype(BF16)
    factor = HEAD_DIM**-0.5 * LOG2E
    for h in range(HEADS // 2):
        g = h // (HEADS // KV_HEADS)
        here = slice(h * HEAD_DIM, (h + 1) * HEAD_DIM)
        q = jnp.concatenate([own_ref[h * TOK : (h + 1) * TOK], other_ref[h * TOK : (h + 1) * TOK]], axis=0)
        q = jnp.concatenate([q, q_doc], axis=1)
        scores = lax.dot_general(q, k_aug[g], NT, preferred_element_type=F32)
        top = jnp.max(scores, axis=1, keepdims=True)
        probs = jnp.exp2((scores - top) * factor).astype(BF16)
        mixed = jnp.dot(probs, v_aug[g], preferred_element_type=F32)
        mixed = (mixed[:, :HEAD_DIM] / mixed[:, HEAD_DIM:]).astype(BF16)
        keep_ref[:, here] = mixed[:TOK]
        send_ref[:, here] = mixed[TOK:]


def selection(route_ref, width):
    chosen = route_ref[0] == 0
    routed = jnp.max(jnp.where(chosen, 1.0, 0.0), axis=1, keepdims=True)
    rows = lax.broadcasted_iota(jnp.int32, (TOK, TOK), 0)
    cols = lax.broadcasted_iota(jnp.int32, (TOK, TOK), 1)
    upto = (cols <= rows).astype(F32).astype(BF16)
    wide = jnp.broadcast_to(routed, (TOK, 128)).astype(BF16)
    slot = jnp.dot(upto, wide, preferred_element_type=F32) - 1.0
    lane = cols.astype(F32)
    hit = (slot == lane) & (lane < float(CAP))
    if width == 2:
        hit = hit | ((slot + float(CAP) == lane) & (slot < float(CAP)))
    return jnp.where(hit & (routed > 0.5), 1.0, 0.0), chosen


def normalized(attn):
    square = jnp.mean(attn * attn, axis=1, keepdims=True)
    inverse = lax.rsqrt(square + EPS)
    return inverse, attn * inverse


def copies(rows, out_ref):
    for i in range(out_ref.shape[0] // CAP):
        out_ref[i * CAP : (i + 1) * CAP, :] = rows


def take(select, rows):
    got = lax.dot_general(select.astype(BF16), rows, TN, preferred_element_type=F32)
    return got[:CAP].astype(BF16)


def send_grads(route_ref, rw_ref, cot_ref, pay_ref):
    select, chosen = selection(route_ref, 1)
    weight = jnp.sum(jnp.where(chosen, rw_ref[0].astype(F32), 0.0), axis=1, keepdims=True)
    weight = jnp.broadcast_to(weight, (TOK, 128)).astype(BF16)
    copies(jnp.concatenate([take(select, cot_ref[0]), take(select, weight)], axis=1), pay_ref)


def send_slots(core_ref, own_ref, other_ref, route_ref, attn_ref, pay_ref):
    core = core_ref[0, 0]
    for side, ref in ((core, own_ref), (1 - core, other_ref)):
        attn_ref[0, :, pl.ds(pl.multiple_of(side * QW, QW), QW)] = ref[...]
    _, scaled = normalized(attn_ref[0].astype(F32))
    select, _ = selection(route_ref, 1)
    copies(take(select, scaled.astype(BF16)), pay_ref)


def expert(x_ref, x2_ref, dy_ref, dy2_ref, w_ref, own_out, other_out, panels, sems):
    depth = panels.shape[2]
    loads = [
        pltpu.make_async_copy(w_ref.at[:, pl.ds(i * depth, depth), :], panels.at[i], sems.at[i])
        for i in range(3)
    ]
    for i in (2, 0, 1):
        loads[i].start()

    def panel(i):
        return panels[i].reshape(D, HALF)

    dy = jnp.concatenate([dy_ref[...], dy2_ref[...]], axis=0)
    x = jnp.concatenate([x_ref[...], x2_ref[...]], axis=0)
    loads[2].wait()
    back = jnp.dot(dy[:, :D], panel(2), preferred_element_type=F32)
    back = back * dy[:, D : D + 1].astype(F32)
    loads[0].wait()
    gate = jnp.dot(x, panel(0), preferred_element_type=F32)
    loads[1].wait()
    up = jnp.dot(x, panel(1), preferred_element_type=F32)
    sg = jax.nn.sigmoid(gate)
    grad_gate = (back * up * sg * (1.0 + gate * (1.0 - sg))).astype(BF16)
    grad_up = (back * gate * sg).astype(BF16)
    part = lax.dot_general(grad_gate, panel(0), NT, preferred_element_type=F32)
    part = part + lax.dot_general(grad_up, panel(1), NT, preferred_element_type=F32)
    half = own_out.shape[0]
    own_out[...] = part[:half]
    other_out[...] = part[half:].astype(BF16)


def finish(attn_ref, route_ref, part_ref, out_ref):
    total = part_ref[0].astype(F32)
    for i in range(1, part_ref.shape[0]):
        total = total + part_ref[i].astype(F32)
    high = total.astype(BF16)
    low = (total - high.astype(F32)).astype(BF16)
    inverse, scaled = normalized(attn_ref[0].astype(F32))
    select, _ = selection(route_ref, 2)
    pair = jnp.concatenate([high.astype(F32), low.astype(F32)], axis=0).astype(BF16)
    d_norm = jnp.dot(
        select[:, : 2 * CAP].astype(BF16), pair, preferred_element_type=F32
    )
    mean = jnp.mean(d_norm * scaled, axis=1, keepdims=True)
    out_ref[0] = (inverse * (d_norm - scaled * mean)).astype(BF16)


def all_to_all(x, axes):
    return lax.all_to_all(x, axes, 0, 0, tiled=True)


def swap(x, axis):
    return lax.ppermute(x, axis, [(0, 1), (1, 0)])


def scalars(*values):
    return jnp.stack([jnp.asarray(v, jnp.int32) for v in values]).reshape(1, -1)


def on_device(q, k, v, doc_ids, routes, route_weight, cotangent, gate_w, up_w, down_w):
    shape = jax.ShapeDtypeStruct
    rows = gate_w.shape[0]
    side, core = lax.axis_index("xl"), lax.axis_index("core")
    peers, chips = lax.axis_size(PEERS), lax.axis_size(CHIPS)

    half = shape((3 * rows, HALF), BF16)
    keep_w, send_w = call(
        pack_weights, (half, half), scalars(side), gate_w, up_w, down_w.T, smem=1
    )
    got_w = swap(send_w, "xl")
    low = jnp.where(side == 0, keep_w, got_w)
    high = jnp.where(side == 0, got_w, keep_w)
    panels = lax.all_gather(jnp.concatenate([low, high]), "z", axis=0, tiled=True)
    panels = panels.reshape(-1, 3 * rows, HALF)

    block = QW + 2 * KW + 8
    packed = shape((block, HEAD_DIM), BF16)
    keep, send = call(
        pack_heads, (packed, packed), scalars(core), q, k, v, doc_ids, smem=1
    )
    got = swap(send, "core")
    kv = jnp.concatenate([keep[QW:], got[QW:]])
    kv = jnp.broadcast_to(kv[None], (chips, *kv.shape)).reshape(-1, HEAD_DIM)
    kv = all_to_all(kv, CHIPS).reshape(-1, block - QW, HEAD_DIM)
    length = kv.shape[0] * TOK

    dy = call(
        send_grads, shape((peers * CAP, D + 128), BF16), routes, route_weight, cotangent
    )
    dy, kv = lax.optimization_barrier((dy, kv))
    own_dy = all_to_all(dy, PEERS)
    other_dy = swap(own_dy, "core")

    mixed = shape((TOK, QW), BF16)
    keep_o, send_o = call(
        attend,
        (mixed, mixed),
        scalars(lax.axis_index(CHIPS) * (2 * TOK), core * TOK),
        keep,
        got,
        kv,
        smem=1,
        flops=16 * TOK * length * QW,
        scratch_shapes=[pltpu.VMEM((2, length, 2 * HEAD_DIM), BF16)] * 2,
    )
    attn, pay = call(
        send_slots,
        (shape((1, TOK, D), BF16), shape((peers * CAP, D), BF16)),
        scalars(core),
        keep_o,
        swap(send_o, "core"),
        routes,
        smem=1,
    )
    own_x = all_to_all(pay, PEERS)
    other_x = swap(own_x, "core")
    own_part, other_part = call(
        expert,
        (shape((peers * CAP, D), F32), shape((peers * CAP, D), BF16)),
        own_x,
        other_x,
        own_dy,
        other_dy,
        panels,
        hbm=1,
        flops=20 * peers * CAP * D * HALF,
        scratch_shapes=[
            pltpu.VMEM((3, panels.shape[0], rows, HALF), BF16),
            pltpu.SemaphoreType.DMA((3,)),
        ],
    )
    part = (own_part + swap(other_part, "core").astype(F32)).astype(BF16)
    part = all_to_all(part, PEERS).reshape(peers, CAP, D)
    d_input = call(finish, shape((1, TOK, D), BF16), attn, routes, part)
    return attn, d_input


def solution(mesh):
    fine = Mesh(mesh.devices.reshape(4, 2, 2, 16, 2), ("y", "xh", "core", "z", "xl"))
    return jax.shard_map(
        on_device,
        mesh=fine,
        in_specs=(
            P(FSDP, CTX, None),
            P(FSDP, CTX, None),
            P(FSDP, CTX, None),
            P(FSDP, CTX),
            P(FSDP, CTX, None),
            P(FSDP, CTX, None),
            P(FSDP, CTX, None),
            P(FSDP, CTX),
            P(FSDP, CTX),
            P(CTX, FSDP),
        ),
        out_specs=(P(FSDP, CTX, None), P(FSDP, CTX, None)),
        check_vma=False,
    )
```

```python
import jax
import jax.numpy as jnp
from jax import lax
from jax.experimental import pallas as pl
from jax.experimental.pallas import tpu as pltpu
from jax.sharding import Mesh
from jax.sharding import PartitionSpec as P

HEADS = 16
KV_HEADS = 4
HEAD_DIM = 128
CAP = 8
TOK = 128
D = 2048
DOCS = 8
EPS = 1e-05
LOG2E = 1.4426950408889634
QW = HEADS * HEAD_DIM // 2
KW = KV_HEADS * HEAD_DIM // 2
FAR = -(2.0**20)
HALF = 256
F32, BF16 = jnp.float32, jnp.bfloat16
CHIPS = ("y", "xh")
PEERS = ("y", "xh", "xl")
CTX = ("y", "xh", "core")
FSDP = ("z", "xl")
NT = (((1,), (1,)), ((), ()))
TN = (((0,), (0,)), ((), ()))


def call(kernel, out_shape, *operands, flops=0, smem=0, hbm=0, **kw):
    nbytes = sum(o.size * o.dtype.itemsize for o in operands)
    nbytes += sum(o.size * o.dtype.itemsize for o in jax.tree.leaves(out_shape))
    vmem = pl.BlockSpec(memory_space=pltpu.VMEM)
    specs = [pl.BlockSpec(memory_space=pltpu.SMEM)] * smem
    specs += [vmem] * (len(operands) - smem - hbm)
    specs += [pl.BlockSpec(memory_space=pl.ANY)] * hbm
    return pl.pallas_call(
        kernel,
        out_shape=out_shape,
        in_specs=specs,
        out_specs=jax.tree.map(lambda _: vmem, out_shape),
        cost_estimate=pl.CostEstimate(flops=flops, bytes_accessed=nbytes, transcendentals=0),
        **kw,
    )(*operands)


def pack_weights(side_ref, gate_ref, up_ref, down_ref, keep_ref, send_ref):
    rows = gate_ref.shape[0]
    rest = gate_ref.shape[1] - HALF

    def write(low_ref, high_ref):
        for i, ref in enumerate((gate_ref, up_ref, down_ref)):
            here = slice(i * rows, (i + 1) * rows)
            low_ref[here, :] = ref[:, :HALF]
            high_ref[here, :] = jnp.concatenate(
                [ref[:, HALF:], jnp.zeros((rows, HALF - rest), BF16)], axis=1
            )

    @pl.when(side_ref[0, 0] == 0)
    def _():
        write(keep_ref, send_ref)

    @pl.when(side_ref[0, 0] != 0)
    def _():
        write(send_ref, keep_ref)


def pack_heads(core_ref, q_ref, k_ref, v_ref, doc_ref, route_ref, keep_ref, send_ref):
    docs = jnp.broadcast_to(doc_ref[...].astype(F32), (4, TOK))
    hits = jnp.where(route_ref[0] == 0, 1.0, 0.0)
    routed = jnp.max(hits, axis=0, keepdims=True)
    rows = lax.broadcasted_iota(jnp.int32, (TOK, TOK), 0)
    cols = lax.broadcasted_iota(jnp.int32, (TOK, TOK), 1)
    upto = jnp.where(rows <= cols, 1.0, 0.0).astype(BF16)
    wide = jnp.broadcast_to(routed, (8, TOK)).astype(BF16)
    count = jnp.dot(wide, upto, preferred_element_type=F32)
    slots = jnp.where(routed > 0.5, count - 1.0, -1.0)
    docs = jnp.concatenate([docs, slots[:4]], axis=0).astype(BF16)
    core = core_ref[0, 0]
    for side, out_ref in ((core, keep_ref), (1 - core, send_ref)):
        row = 0
        for ref, width in ((q_ref, QW), (k_ref, KW), (v_ref, KW)):
            for h in range(width // HEAD_DIM):
                start = pl.multiple_of(side * width + h * HEAD_DIM, HEAD_DIM)
                out_ref[row : row + TOK, :] = ref[0, :, pl.ds(start, HEAD_DIM)]
                row += TOK
        out_ref[row:, :] = docs


def spread(keep_ref, got_ref, out_ref):
    for i in range(out_ref.shape[0]):
        out_ref[i, 0] = keep_ref[QW:, :]
        out_ref[i, 1] = got_ref[QW:, :]


def attend(base_ref, own_ref, other_ref, kv_ref, keep_ref, send_ref, pay_ref, k_aug, v_aug):
    length = k_aug.shape[1]
    heads = KW // HEAD_DIM
    docs = kv_ref[:, 2 * heads * TOK :, :].astype(F32)
    lane = lax.broadcasted_iota(jnp.int32, (1, 128), 1)
    first = jnp.zeros((1, 128), F32)
    after = jnp.where(lane < DOCS, float(length), 0.0)
    for d in range(1, DOCS):
        below = jnp.sum(jnp.where(docs < float(d), 1.0, 0.0), axis=0)
        count = jnp.sum(below[:1], axis=1, keepdims=True)
        first = jnp.where(lane == d, count, first)
        after = jnp.where(lane == d - 1, count, after)
    turn = base_ref[0, 1]
    spot = (lax.broadcasted_iota(jnp.int32, (length, 128), 0) ^ turn).astype(F32)
    inside = (spot >= first) & (spot < after)
    k_doc = jnp.where(inside, 0.0, FAR).astype(BF16)
    for g in range(heads):
        here = slice(g * TOK, (g + 1) * TOK)
        there = slice((heads + g) * TOK, (heads + g + 1) * TOK)
        k_aug[g, :, :HEAD_DIM] = kv_ref[:, here, :].reshape(length, HEAD_DIM)
        k_aug[g, :, HEAD_DIM:] = k_doc
        v_aug[g, :, :HEAD_DIM] = kv_ref[:, there, :].reshape(length, HEAD_DIM)
        v_aug[g, :, HEAD_DIM:] = jnp.ones((length, HEAD_DIM), BF16)
    mine = lax.broadcasted_iota(jnp.int32, (2 * TOK, 128), 0) ^ turn
    mine = (mine + base_ref[0, 0]).astype(F32)
    q_doc = jnp.where((mine >= first) & (mine < after), 1.0, 0.0).astype(BF16)
    factor = HEAD_DIM**-0.5 * LOG2E
    place = lax.broadcasted_iota(jnp.int32, (CAP, TOK), 0).astype(F32)
    picks = []
    for ref in (own_ref, other_ref):
        slots = ref[QW + 2 * KW :, :].astype(F32)[4:5]
        picks.append(jnp.where(place == slots, 1.0, 0.0).astype(BF16))
    chosen = [[], []]
    for h in range(HEADS // 2):
        g = h // (HEADS // KV_HEADS)
        here = slice(h * HEAD_DIM, (h + 1) * HEAD_DIM)
        rows = slice(h * TOK, (h + 1) * TOK)
        q = jnp.concatenate([own_ref[rows], other_ref[rows]], axis=0)
        q = jnp.concatenate([q, q_doc], axis=1)
        scores = lax.dot_general(q, k_aug[g], NT, preferred_element_type=F32)
        top = jnp.max(scores, axis=1, keepdims=True)
        probs = jnp.exp2((scores - top) * factor).astype(BF16)
        mixed = jnp.dot(probs, v_aug[g], preferred_element_type=F32)
        mixed = (mixed[:, :HEAD_DIM] / mixed[:, HEAD_DIM:]).astype(BF16)
        keep_ref[:, here] = mixed[:TOK]
        send_ref[:, here] = mixed[TOK:]
        for i, part in enumerate((mixed[:TOK], mixed[TOK:])):
            got = jnp.dot(picks[i], part, preferred_element_type=F32)
            chosen[i].append(got.astype(BF16))
    copies(jnp.concatenate(chosen[0] + chosen[1], axis=1), pay_ref)


def selection(route_ref, width):
    chosen = route_ref[0] == 0
    routed = jnp.max(jnp.where(chosen, 1.0, 0.0), axis=1, keepdims=True)
    rows = lax.broadcasted_iota(jnp.int32, (TOK, TOK), 0)
    cols = lax.broadcasted_iota(jnp.int32, (TOK, TOK), 1)
    upto = (cols <= rows).astype(F32).astype(BF16)
    wide = jnp.broadcast_to(routed, (TOK, 128)).astype(BF16)
    slot = jnp.dot(upto, wide, preferred_element_type=F32) - 1.0
    lane = cols.astype(F32)
    hit = (slot == lane) & (lane < float(CAP))
    if width == 2:
        hit = hit | ((slot + float(CAP) == lane) & (slot < float(CAP)))
    return jnp.where(hit & (routed > 0.5), 1.0, 0.0), chosen


def normalized(attn):
    square = jnp.mean(attn * attn, axis=1, keepdims=True)
    inverse = lax.rsqrt(square + EPS)
    return inverse, attn * inverse


def copies(rows, out_ref):
    for i in range(out_ref.shape[0] // CAP):
        out_ref[i * CAP : (i + 1) * CAP, :] = rows


def take(select, rows):
    got = lax.dot_general(select.astype(BF16), rows, TN, preferred_element_type=F32)
    return got[:CAP].astype(BF16)


def send_grads(route_ref, rw_ref, cot_ref, pay_ref):
    select, chosen = selection(route_ref, 1)
    weight = jnp.sum(jnp.where(chosen, rw_ref[0].astype(F32), 0.0), axis=1, keepdims=True)
    weight = jnp.broadcast_to(weight, (TOK, 128)).astype(BF16)
    copies(jnp.concatenate([take(select, cot_ref[0]), take(select, weight)], axis=1), pay_ref)


def join(core_ref, own_ref, other_ref, attn_ref):
    core = core_ref[0, 0]
    for side, ref in ((core, own_ref), (1 - core, other_ref)):
        attn_ref[0, :, pl.ds(pl.multiple_of(side * QW, QW), QW)] = ref[...]


def expert(ids_ref, x_ref, x2_ref, dy_ref, dy2_ref, w_ref, own_out, other_out, panels, sems):
    core, side = ids_ref[0, 0], ids_ref[0, 1]
    depth = panels.shape[3]
    loads = {}
    for i in (2, 0, 1):
        for s in range(2):
            loads[i, s] = pltpu.make_async_copy(
                w_ref.at[:, side ^ s, pl.ds(i * depth, depth), :],
                panels.at[i, :, s],
                sems.at[i, s],
            )
            loads[i, s].start()

    def panel(i, half):
        blocks = panels.shape[1] // 2
        start = pl.multiple_of(half * blocks, blocks)
        return panels[i, pl.ds(start, blocks)].reshape(QW, HALF)

    def ready(i):
        loads[i, 0].wait()
        loads[i, 1].wait()

    sides = (core, 1 - core)
    attn = (
        jnp.concatenate([x_ref[:, :QW], x_ref[:, QW:]], axis=0).astype(F32),
        jnp.concatenate([x2_ref[:, QW:], x2_ref[:, :QW]], axis=0).astype(F32),
    )
    square = sum(jnp.sum(a * a, axis=1, keepdims=True) for a in attn) * (1.0 / D)
    inverse = lax.rsqrt(square + EPS)
    x = [(a * inverse).astype(BF16) for a in attn]
    dy = jnp.concatenate([dy_ref[...], dy2_ref[...]], axis=0)
    ready(2)
    back = jnp.dot(dy[:, :D], panels[2].reshape(D, HALF), preferred_element_type=F32)
    back = back * dy[:, D : D + 1].astype(F32)

    def forward(i):
        ready(i)
        first = jnp.dot(x[0], panel(i, sides[0]), preferred_element_type=F32)
        return first + jnp.dot(x[1], panel(i, sides[1]), preferred_element_type=F32)

    gate, up = forward(0), forward(1)
    sg = jax.nn.sigmoid(gate)
    grad_gate = (back * up * sg * (1.0 + gate * (1.0 - sg))).astype(BF16)
    grad_up = (back * gate * sg).astype(BF16)
    rows = own_out.shape[0]
    for half in range(2):
        part = lax.dot_general(grad_gate, panel(0, half), NT, preferred_element_type=F32)
        part = part + lax.dot_general(
            grad_up, panel(1, half), NT, preferred_element_type=F32
        )
        here = slice(half * QW, (half + 1) * QW)
        own_out[:, here] = part[:rows]
        other_out[:, here] = part[rows:].astype(BF16)


def finish(attn_ref, route_ref, part_ref, out_ref):
    total = part_ref[0].astype(F32)
    for i in range(1, part_ref.shape[0]):
        total = total + part_ref[i].astype(F32)
    high = total.astype(BF16)
    low = (total - high.astype(F32)).astype(BF16)
    inverse, scaled = normalized(attn_ref[0].astype(F32))
    select, _ = selection(route_ref, 2)
    pair = jnp.concatenate([high.astype(F32), low.astype(F32)], axis=0).astype(BF16)
    d_norm = jnp.dot(
        select[:, : 2 * CAP].astype(BF16), pair, preferred_element_type=F32
    )
    mean = jnp.mean(d_norm * scaled, axis=1, keepdims=True)
    out_ref[0] = (inverse * (d_norm - scaled * mean)).astype(BF16)


def all_to_all(x, axes):
    return lax.all_to_all(x, axes, 0, 0, tiled=True)


def swap(x, axis):
    return lax.ppermute(x, axis, [(0, 1), (1, 0)])


def scalars(*values):
    return jnp.stack([jnp.asarray(v, jnp.int32) for v in values]).reshape(1, -1)


def on_device(q, k, v, doc_ids, routes, route_weight, cotangent, gate_w, up_w, down_w):
    shape = jax.ShapeDtypeStruct
    rows = gate_w.shape[0]
    side, core = lax.axis_index("xl"), lax.axis_index("core")
    peers, chips = lax.axis_size(PEERS), lax.axis_size(CHIPS)

    half = shape((3 * rows, HALF), BF16)
    keep_w, send_w = call(
        pack_weights, (half, half), scalars(side), gate_w, up_w, down_w.T, smem=1
    )
    got_w = swap(send_w, "xl")
    block = QW + 2 * KW + 8
    packed = shape((block, HEAD_DIM), BF16)
    keep, send = call(
        pack_heads,
        (packed, packed),
        scalars(core),
        q,
        k,
        v,
        doc_ids,
        jnp.swapaxes(routes, 1, 2),
        smem=1,
    )
    keep, got_w = lax.optimization_barrier((keep, got_w))
    panels = lax.all_gather(jnp.concatenate([keep_w, got_w]), "z", axis=0, tiled=True)
    panels = panels.reshape(-1, 2, 3 * rows, HALF)

    got = swap(send, "core")
    kv = call(spread, shape((chips, 2, block - QW, HEAD_DIM), BF16), keep, got)
    kv = all_to_all(kv.reshape(-1, HEAD_DIM), CHIPS).reshape(-1, block - QW, HEAD_DIM)
    length = kv.shape[0] * TOK

    dy = call(
        send_grads, shape((peers * CAP, D + 128), BF16), routes, route_weight, cotangent
    )
    dy, kv = lax.optimization_barrier((dy, kv))
    own_dy = all_to_all(dy, PEERS)
    other_dy = swap(own_dy, "core")

    mixed = shape((TOK, QW), BF16)
    keep_o, send_o, pay = call(
        attend,
        (mixed, mixed, shape((peers * CAP, D), BF16)),
        scalars(lax.axis_index(CHIPS) * (2 * TOK), core * TOK),
        keep,
        got,
        kv,
        smem=1,
        flops=16 * TOK * length * QW,
        scratch_shapes=[pltpu.VMEM((2, length, 2 * HEAD_DIM), BF16)] * 2,
    )
    own_x = all_to_all(pay, PEERS)
    attn = call(
        join, shape((1, TOK, D), BF16), scalars(core), keep_o, swap(send_o, "core"), smem=1
    )
    other_x = swap(own_x, "core")
    own_part, other_part = call(
        expert,
        (shape((peers * CAP, D), F32), shape((peers * CAP, D), BF16)),
        scalars(core, side),
        own_x,
        other_x,
        own_dy,
        other_dy,
        panels,
        smem=1,
        hbm=1,
        flops=20 * peers * CAP * D * HALF,
        scratch_shapes=[
            pltpu.VMEM((3, panels.shape[0], 2, rows, HALF), BF16),
            pltpu.SemaphoreType.DMA((3, 2)),
        ],
    )
    part = (own_part + swap(other_part, "core").astype(F32)).astype(BF16)
    part = all_to_all(part, PEERS).reshape(peers, CAP, D)
    d_input = call(finish, shape((1, TOK, D), BF16), attn, routes, part)
    return attn, d_input


def solution(mesh):
    fine = Mesh(mesh.devices.reshape(4, 2, 2, 16, 2), ("y", "xh", "core", "z", "xl"))
    return jax.shard_map(
        on_device,
        mesh=fine,
        in_specs=(
            P(FSDP, CTX, None),
            P(FSDP, CTX, None),
            P(FSDP, CTX, None),
            P(FSDP, CTX),
            P(FSDP, CTX, None),
            P(FSDP, CTX, None),
            P(FSDP, CTX, None),
            P(FSDP, CTX),
            P(FSDP, CTX),
            P(CTX, FSDP),
        ),
        out_specs=(P(FSDP, CTX, None), P(FSDP, CTX, None)),
        check_vma=False,
    )
```
